32 devices in a mesh: tensor: 2 (over core), outer: 4 (over z), inter: 4 (over y, x).
Axes of the slice: x: 2, y: 2, z: 4, core: 2. Of those that a mesh axis runs over, the one named last changes fastest.
Arguments:
- features: bfloat16 [4096, 5120], P(('outer', 'inter')), may hold values from -6 to 6
- attn_weights: bfloat16 [16, 20, 256, 256], P(('outer', 'inter'), 'tensor'), may hold values from 0 to 0.0078125
- out_grad: bfloat16 [4096, 2560], P(('outer', 'inter'), 'tensor'), may hold values from -192 to 192
- storm_index: int32 [16, 96], P(('outer', 'inter')), may hold values from 0 to 255, as said below
- w_value: bfloat16 [5120, 2560], P(('outer', 'inter'), 'tensor'), may hold values from -0.078125 to 0.078125
Outputs:
- grad_input: bfloat16 [4096, 5120], P(('outer', 'inter'), 'tensor')
- grad_weight: bfloat16 [5120, 2560], P(('outer', 'inter'), 'tensor')
The draws below stay inside these ranges and needn't reach their ends.
Inputs may be any that keep to these rules, and one draw needn't show every extreme that they name: `storm_index`: each row holds 96 different token positions of one window of 256 tokens.
All inputs are finite; a program needn't handle non-finite values.
Results may differ from the reference program's by a relative error of at most 0.019.
Values may be sent and summed in bfloat16 or wider, within the bound.
A program may use at most 128 MiB of HBM per device.

```python
import jax
import jax.numpy as jnp
from jax import lax

D = 5120
HEADS = 20
HEAD_DIM = 128
PATCHES = 256
HW = 2560
TOK_DEV = 256
STORM = 96
WINDOWS = 16
TOKENS = 4096
N_TENSOR = 2
N_OUTER = 4
N_INTER = 4


def draw_storm_index(key, part):
    keys = jax.random.split(jax.random.fold_in(key, 17), WINDOWS)

    def one_window(window_key):
        order = jax.random.permutation(window_key, jnp.arange(PATCHES, dtype=jnp.int32))
        return order[:STORM]
    return jax.vmap(one_window)(keys).astype(jnp.int32)


def spiked(drawn, own_key, source, target, blocks, factor):
    owner, partner = [(jnp.arange(drawn.shape[dim]) // (drawn.shape[dim] // blocks)).reshape([-1 if axis == dim else 1 for axis in range(drawn.ndim)]) for dim in (source, target)]
    chosen = jax.random.permutation(own_key, blocks)[partner]
    strong = (owner == chosen) | (owner == (partner + blocks // 2) % blocks)
    return jnp.where(strong, factor * drawn, drawn)


def shard_levels(rng, shape, cuts, low, top_value):
    factor_of, own = 1.0, jax.random.fold_in(rng, 6)
    for position, shards_of in cuts:
        draws = jnp.exp(jax.random.uniform(jax.random.fold_in(own, position), (shards_of,), jnp.float32, low / len(cuts), top_value / len(cuts)))
        factor_of = factor_of * jnp.repeat(draws, shape[position] // shards_of).reshape([-1 if axis == position else 1 for axis in range(len(shape))])
    return factor_of


def normal_values(rng, shape, deviation, limit, pieces=(), kind=jnp.bfloat16):
    result = jax.random.normal(rng, shape, jnp.float32) * deviation
    if len(pieces) > 0:
        result = shard_levels(rng, shape, pieces, -0.22, 0.18) * result
    return jnp.clip(result, min=-limit, max=limit).astype(kind)


def bell_draw_with(rng, shape, spread, most, shards, heavy, held_as=jnp.bfloat16):
    drawn = spread * jax.random.normal(rng, shape, jnp.float32)
    if shards:
        drawn = drawn * shard_levels(rng, shape, shards, -0.22, 0.18)
    return jnp.clip(spiked(drawn, jax.random.fold_in(rng, 3), *heavy), -most, most).astype(held_as)


def setup_inputs(seed: int = 0) -> dict:
    key_list = jax.random.split(jax.random.key(seed), 6)
    return {
        "features": bell_draw_with(key_list[0], (TOKENS, D), 1.0, 6.0, ((0, 16),), (0, 1, 16, 2.0)),
        "attn_weights": jnp.clip(0.0078125 * jax.random.uniform(key_list[1], (WINDOWS, HEADS, PATCHES, PATCHES), jnp.float32) ** shard_levels(key_list[1], (WINDOWS, HEADS, PATCHES, PATCHES), ((0, 16), (1, 2)), -0.2, 0.2), 0.0, 0.0078125).astype(jnp.bfloat16),
        "out_grad": normal_values(key_list[2], (TOKENS, HW), 32.0, 192.0, ((0, 16), (1, 2))),
        "storm_index": draw_storm_index(jax.random.fold_in(key_list[5], 71), 0),
        "w_value": normal_values(key_list[4], (D, HW), D ** -0.5, 0.078125, ((0, 16), (1, 2))),
    }


def reference(features, attn_weights, out_grad, storm_index, w_value):
    positions = jnp.arange(PATCHES, dtype=jnp.int32)
    in_storm = jnp.any(storm_index[:, :, None] == positions[None, None, :], axis=1)
    masked = out_grad.astype(jnp.float32).reshape(WINDOWS, PATCHES, HEADS, HEAD_DIM)
    masked = masked * in_storm[:, :, None, None].astype(jnp.float32)
    value_grad = jnp.einsum("whij,wihd->wjhd", attn_weights.astype(jnp.float32), masked)
    value_grad = value_grad.astype(jnp.bfloat16).reshape(TOKENS, HW)

    split = HW // N_TENSOR
    total = jnp.zeros((TOKENS, D), jnp.float32)
    for block in range(N_TENSOR):
        left = value_grad[:, block * split:(block + 1) * split].astype(jnp.float32)
        right = w_value[:, block * split:(block + 1) * split].astype(jnp.float32)
        partial_k = jnp.dot(left, right.T, preferred_element_type=jnp.float32).astype(jnp.bfloat16)
        total = total + lax.optimization_barrier(partial_k).astype(jnp.float32)
    grad_input = total.astype(jnp.bfloat16)

    def rank_term(rank):
        start = (rank * TOK_DEV).astype(jnp.int32)
        rows = lax.dynamic_slice_in_dim(features, start, TOK_DEV, 0).astype(jnp.float32)
        values = lax.dynamic_slice_in_dim(value_grad, start, TOK_DEV, 0).astype(jnp.float32)
        term = jnp.dot(rows.T, values, preferred_element_type=jnp.float32).astype(jnp.bfloat16)
        return lax.optimization_barrier(term).astype(jnp.float32)

    def pod_sum(inner):
        def add_outer(outer, acc):
            return acc + rank_term(outer * N_INTER + inner)
        acc = lax.fori_loop(0, N_OUTER, add_outer, jnp.zeros((D, HW), jnp.float32))
        return lax.optimization_barrier(acc.astype(jnp.bfloat16)).astype(jnp.float32)

    def add_inner(inner, acc):
        return acc + pod_sum(inner)

    summed = lax.fori_loop(0, N_INTER, add_inner, jnp.zeros((D, HW), jnp.float32))
    grad_weight = (summed / (N_OUTER * N_INTER)).astype(jnp.bfloat16)
    return grad_input, grad_weight
```

```python
import jax
import jax.numpy as jnp
from jax import lax
from jax.sharding import PartitionSpec as P


def shifted(x, axis, count, step):
    if count & (count - 1) == 0:
        pairs = [(k, k ^ step) for k in range(count)]
    else:
        pairs = [(k, (k + step) % count) for k in range(count)]
    return lax.ppermute(x, axis, pairs)


def peer(me, count, step):
    return me ^ step if count & (count - 1) == 0 else (me + step) % count


def origin(me, count, step):
    return me ^ step if count & (count - 1) == 0 else (me - step) % count


def local(features, attn_weights, out_grad, storm_index, w_value):
    windows, heads_local, patches, _ = attn_weights.shape
    tokens = features.shape[0]
    width = out_grad.shape[1]
    head_size = width // heads_local
    rows = w_value.shape[0]
    no, ni, nt = lax.axis_size("outer"), lax.axis_size("inter"), lax.axis_size("tensor")
    me, core = lax.axis_index("inter"), lax.axis_index("tensor")
    half = no // nt
    f32, bf16 = jnp.float32, jnp.bfloat16

    w_all = lax.all_gather(w_value, "outer", axis=0, tiled=True)
    f_view = features.reshape(tokens, no, ni, rows)

    def f_block(i):
        part = lax.dynamic_slice(
            f_view, (0, core * half, i, 0), (tokens, half, 1, rows)
        )
        return part.reshape(tokens, half * rows)

    positions = lax.broadcasted_iota(jnp.int32, (1, 1, patches), 2)
    in_storm = jnp.any(storm_index[:, :, None] == positions, axis=1)
    masked = out_grad.reshape(windows, patches, heads_local, head_size)
    masked = masked * in_storm[:, :, None, None].astype(out_grad.dtype)
    value_grad = jnp.einsum(
        "whij,wihd->wjhd", attn_weights, masked, preferred_element_type=f32
    )
    value_grad = value_grad.astype(bf16).reshape(tokens, width)

    f_parts = [f_block(me)]
    v_parts = [value_grad]
    for step in range(1, ni):
        f_parts.append(shifted(f_block(peer(me, ni, step)), "inter", ni, step))
        v_parts.append(shifted(value_grad, "inter", ni, step))
    v_all = jnp.concatenate(v_parts, axis=0)
    f_mine = jnp.concatenate(f_parts, axis=0)
    ring = [(k, (k + 1) % nt) for k in range(nt)]
    shares = [f_mine]
    for _ in range(1, nt):
        shares.append(lax.ppermute(shares[-1], "tensor", ring))

    term = jnp.zeros((nt, half * rows, width), bf16)
    for back, share in enumerate(shares):
        product = lax.dot_general(
            share, v_all, (((0,), (0,)), ((), ())), preferred_element_type=f32
        ).astype(bf16)
        term = lax.dynamic_update_slice(term, product[None], ((core - back) % nt, 0, 0))
    summed = lax.psum_scatter(
        term.reshape(no * rows, width), "outer", scatter_dimension=0, tiled=True
    )
    grad_weight = (summed.astype(f32) / (no * ni)).astype(bf16)

    part = lax.dot_general(
        v_all, w_all, (((1,), (1,)), ((), ())), preferred_element_type=f32
    ).astype(bf16)
    part = part.reshape(ni * tokens, nt, half * rows)

    def share_of(t):
        return lax.dynamic_slice(
            part, (0, t, 0), (ni * tokens, 1, half * rows)
        ).reshape(ni * tokens, half * rows)

    total = share_of(core).astype(f32)
    for step in range(1, nt):
        pairs = [(k, (k + step) % nt) for k in range(nt)]
        total = total + lax.ppermute(share_of((core + step) % nt), "tensor", pairs).astype(f32)
    total = total.astype(bf16).reshape(ni, tokens, half, rows)
    out = jnp.zeros((tokens, half, ni, rows), bf16)
    for step in range(ni):
        back = (-step) % ni if ni & (ni - 1) else step
        got = total[step] if step == 0 else shifted(total[step], "inter", ni, back)
        source = peer(me, ni, step) if step else me
        out = lax.dynamic_update_slice(out, got[:, :, None, :], (0, 0, source, 0))
    return (out.reshape(tokens, half * ni * rows), grad_weight)


def solution(mesh):
    in_specs = (
        P(("outer", "inter"), None),
        P(("outer", "inter"), "tensor", None, None),
        P(("outer", "inter"), "tensor"),
        P(("outer", "inter"), None),
        P(("outer", "inter"), "tensor"),
    )
    out_specs = (P(("outer", "inter"), "tensor"), P(("outer", "inter"), "tensor"))
    return jax.shard_map(local, mesh=mesh, in_specs=in_specs, out_specs=out_specs, check_vma=False)
```

```python
import jax
import jax.numpy as jnp
from jax import lax
from jax.sharding import PartitionSpec as P


def shifted(x, axis, count, step):
    if count & (count - 1) == 0:
        pairs = [(k, k ^ step) for k in range(count)]
    else:
        pairs = [(k, (k + step) % count) for k in range(count)]
    return lax.ppermute(x, axis, pairs)


def peer(me, count, step):
    return me ^ step if count & (count - 1) == 0 else (me + step) % count


def local(features, attn_weights, out_grad, storm_index, w_value):
    windows, heads_local, patches, _ = attn_weights.shape
    tokens = features.shape[0]
    width = out_grad.shape[1]
    head_size = width // heads_local
    rows = w_value.shape[0]
    no, ni, nt = lax.axis_size("outer"), lax.axis_size("inter"), lax.axis_size("tensor")
    me, core, place = lax.axis_index("inter"), lax.axis_index("tensor"), lax.axis_index("outer")
    half = no // nt
    f32, bf16 = jnp.float32, jnp.bfloat16

    positions = lax.broadcasted_iota(jnp.int32, (1, 1, patches), 2)
    in_storm = jnp.any(storm_index[:, :, None] == positions, axis=1)
    masked = out_grad.reshape(windows, patches, heads_local, head_size)
    masked = masked * in_storm[:, :, None, None].astype(out_grad.dtype)
    value_grad = jnp.einsum(
        "whij,wihd->wjhd", attn_weights, masked, preferred_element_type=f32
    )
    value_grad = value_grad.astype(bf16).reshape(tokens, width)

    value_grad, features = lax.optimization_barrier((value_grad, features))

    if ni == 4:
        cut = width // 2
        v_one = shifted(value_grad, "inter", ni, 1)
        v_two = shifted(value_grad, "inter", ni, 2)
        far_a = shifted(v_one[:, :cut], "inter", ni, 2)
        far_b = shifted(v_two[:, cut:], "inter", ni, 1)
        v_far = jnp.concatenate([far_a, far_b], axis=1)
        v_parts = [value_grad, v_one, v_two, v_far]
    else:
        v_parts = [value_grad] + [shifted(value_grad, "inter", ni, s) for s in range(1, ni)]
    v_all = jnp.concatenate(v_parts, axis=0)

    f_view = features.reshape(tokens, no, ni, rows)

    def f_block(i):
        part = lax.dynamic_slice(
            f_view, (0, core * half, i, 0), (tokens, half, 1, rows)
        )
        return part.reshape(tokens, half * rows)

    ups, downs = [w_value], [w_value]

    def hop_on(hop):
        right = [(k, k + 1) for k in range(hop - 1, no - 1)]
        left = [(k, k - 1) for k in range(1, no - hop + 1)]
        ups.append(lax.ppermute(ups[-1], "outer", right))
        downs.append(lax.ppermute(downs[-1], "outer", left))

    hop_on(1)
    ups[1], downs[1], _ = lax.optimization_barrier((ups[1], downs[1], v_parts[1]))
    hop_on(2)

    f_parts = [f_block(me)] + [f_block(peer(me, ni, step)) for step in range(1, ni)]
    f_parts, _ = lax.optimization_barrier((f_parts, v_parts[1:3]))
    for step in range(1, ni):
        f_parts[step] = shifted(f_parts[step], "inter", ni, step)
    f_parts, _ = lax.optimization_barrier((f_parts, ups[1:2] + downs[1:2]))
    f_mine = jnp.concatenate(f_parts, axis=0)
    ring = [(k, (k + 1) % nt) for k in range(nt)]
    shares = [f_mine]
    for _ in range(1, nt):
        shares.append(lax.ppermute(shares[-1], "tensor", ring))
    ups[2], downs[2], _ = lax.optimization_barrier((ups[2], downs[2], shares[0]))
    for hop in range(3, no):
        hop_on(hop)
    pieces = []
    for t in range(nt):
        piece = shares[0]
        for back in range(1, nt):
            piece = jnp.where((core - back) % nt == t, shares[back], piece)
        pieces.append(piece)
    f_all = jnp.concatenate(pieces, axis=1)

    term = lax.dot_general(
        f_all, v_all, (((0,), (0,)), ((), ())), preferred_element_type=f32
    ).astype(bf16).reshape(no, rows, width)

    ups[-1], downs[-1], _ = lax.optimization_barrier((ups[-1], downs[-1], term))
    w_all = jnp.zeros((no, rows, width), bf16)
    for hop in range(no):
        block = w_value if hop == 0 else jnp.where(place >= hop, ups[hop], downs[no - hop])
        w_all = lax.dynamic_update_slice(w_all, block[None], ((place - hop) % no, 0, 0))

    def block_of(o):
        return lax.dynamic_index_in_dim(term, jnp.clip(o, 0, no - 1), 0, keepdims=False)

    up, down = None, None
    for step in range(no - 1):
        add_up, add_down = block_of(place + no - 1 - step), block_of(place - no + 1 + step)
        if step:
            add_up = (up.astype(f32) + add_up.astype(f32)).astype(bf16)
            add_down = (down.astype(f32) + add_down.astype(f32)).astype(bf16)
        up = lax.ppermute(add_up, "outer", [(k, k + 1) for k in range(min(step + 1, no - 1))])
        down = lax.ppermute(
            add_down, "outer", [(k, k - 1) for k in range(max(1, no - 1 - step), no)]
        )
    summed = block_of(place).astype(f32) + up.astype(f32) + down.astype(f32)
    grad_weight = (summed / (no * ni)).astype(bf16)

    def share_of(t):
        w_share = lax.dynamic_slice(w_all, (t * half, 0, 0), (half, rows, width))
        return lax.dot_general(
            v_all,
            w_share.reshape(half * rows, width),
            (((1,), (1,)), ((), ())),
            preferred_element_type=f32,
        ).astype(bf16)

    total = 0.0
    for step in list(range(1, nt)) + [0]:
        share = share_of((core + step) % nt)
        if step:
            share = lax.ppermute(share, "tensor", [(k, (k + step) % nt) for k in range(nt)])
        total = total + share.astype(f32)
    total = total.astype(bf16).reshape(ni, tokens, half, rows)
    out = jnp.zeros((tokens, half, ni, rows), bf16)
    for step in range(ni):
        back = (-step) % ni if ni & (ni - 1) else step
        got = total[step] if step == 0 else shifted(total[step], "inter", ni, back)
        source = peer(me, ni, step) if step else me
        out = lax.dynamic_update_slice(out, got[:, :, None, :], (0, 0, source, 0))
    return (out.reshape(tokens, half * ni * rows), grad_weight)


def solution(mesh):
    in_specs = (
        P(("outer", "inter"), None),
        P(("outer", "inter"), "tensor", None, None),
        P(("outer", "inter"), "tensor"),
        P(("outer", "inter"), None),
        P(("outer", "inter"), "tensor"),
    )
    out_specs = (P(("outer", "inter"), "tensor"), P(("outer", "inter"), "tensor"))

    return jax.shard_map(local, mesh=mesh, in_specs=in_specs, out_specs=out_specs, check_vma=False)
```

```python
import jax
import jax.numpy as jnp
from jax import lax
from jax.sharding import PartitionSpec as P


def shifted(x, axis, count, step):
    if count & (count - 1) == 0:
        pairs = [(k, k ^ step) for k in range(count)]
    else:
        pairs = [(k, (k + step) % count) for k in range(count)]
    return lax.ppermute(x, axis, pairs)


def peer(me, count, step):
    return me ^ step if count & (count - 1) == 0 else (me + step) % count


def local(features, attn_weights, out_grad, storm_index, w_value):
    windows, heads_local, patches, _ = attn_weights.shape
    tokens = features.shape[0]
    width = out_grad.shape[1]
    head_size = width // heads_local
    rows = w_value.shape[0]
    no, ni, nt = lax.axis_size("outer"), lax.axis_size("inter"), lax.axis_size("tensor")
    me, core, place = lax.axis_index("inter"), lax.axis_index("tensor"), lax.axis_index("outer")
    half = no // nt
    f32, bf16 = jnp.float32, jnp.bfloat16

    positions = lax.broadcasted_iota(jnp.int32, (1, 1, patches), 2)
    in_storm = jnp.any(storm_index[:, :, None] == positions, axis=1)
    masked = out_grad.reshape(windows, patches, heads_local, head_size)
    masked = masked * in_storm[:, :, None, None].astype(out_grad.dtype)
    value_grad = jnp.einsum(
        "whij,wihd->wjhd", attn_weights, masked, preferred_element_type=f32
    )
    value_grad = value_grad.astype(bf16).reshape(tokens, width)

    value_grad, features = lax.optimization_barrier((value_grad, features))

    if ni == 4:
        cut = width // 2
        v_one = shifted(value_grad, "inter", ni, 1)
        v_two = shifted(value_grad, "inter", ni, 2)
        far_a = shifted(v_one[:, :cut], "inter", ni, 2)
        far_b = shifted(v_two[:, cut:], "inter", ni, 1)
        v_far = jnp.concatenate([far_a, far_b], axis=1)
        v_parts = [value_grad, v_one, v_two, v_far]
    else:
        v_parts = [value_grad] + [shifted(value_grad, "inter", ni, s) for s in range(1, ni)]
    v_all = jnp.concatenate(v_parts, axis=0)

    f_view = features.reshape(tokens, no, ni, rows)

    def f_block(i):
        part = lax.dynamic_slice(
            f_view, (0, core * half, i, 0), (tokens, half, 1, rows)
        )
        return part.reshape(tokens, half * rows)

    ups, downs = [w_value], [w_value]

    def hop_on(hop):
        right = [(k, k + 1) for k in range(hop - 1, no - 1)]
        left = [(k, k - 1) for k in range(1, no - hop + 1)]
        ups.append(lax.ppermute(ups[-1], "outer", right))
        downs.append(lax.ppermute(downs[-1], "outer", left))

    hop_on(1)
    ups[1], downs[1], _ = lax.optimization_barrier((ups[1], downs[1], v_parts[1]))
    hop_on(2)

    f_parts = [f_block(me)] + [f_block(peer(me, ni, step)) for step in range(1, ni)]
    f_parts, _ = lax.optimization_barrier((f_parts, v_parts[1:3]))
    for step in range(1, ni):
        f_parts[step] = shifted(f_parts[step], "inter", ni, step)
    f_parts, _ = lax.optimization_barrier((f_parts, ups[1:2] + downs[1:2]))
    f_mine = jnp.concatenate(f_parts, axis=0)
    ring = [(k, (k + 1) % nt) for k in range(nt)]
    shares = [f_mine]
    for _ in range(1, nt):
        shares.append(lax.ppermute(shares[-1], "tensor", ring))
    pieces = []
    for t in range(nt):
        piece = shares[0]
        for back in range(1, nt):
            piece = jnp.where((core - back) % nt == t, shares[back], piece)
        pieces.append(piece)
    f_all = jnp.concatenate(pieces, axis=1)

    term = lax.dot_general(
        f_all, v_all, (((0,), (0,)), ((), ())), preferred_element_type=f32
    ).astype(bf16).reshape(no, rows, width)

    ups[2], downs[2], _ = lax.optimization_barrier((ups[2], downs[2], term))
    for hop in range(3, no):
        hop_on(hop)
    w_all = jnp.zeros((no, rows, width), bf16)
    for hop in range(no):
        block = w_value if hop == 0 else jnp.where(place >= hop, ups[hop], downs[no - hop])
        w_all = lax.dynamic_update_slice(w_all, block[None], ((place - hop) % no, 0, 0))

    def reduced(left_edge, columns):
        def block_of(o):
            at = (jnp.clip(o, 0, no - 1), 0, left_edge)
            return lax.dynamic_slice(term, at, (1, rows, columns)).reshape(rows, columns)

        up, down = None, None
        for step in range(no - 1):
            add_up, add_down = block_of(place + no - 1 - step), block_of(place - no + 1 + step)
            if step:
                add_up = (up.astype(f32) + add_up.astype(f32)).astype(bf16)
                add_down = (down.astype(f32) + add_down.astype(f32)).astype(bf16)
            right = [(k, k + 1) for k in range(min(step + 1, no - 1))]
            left = [(k, k - 1) for k in range(max(1, no - 1 - step), no)]
            up = lax.ppermute(add_up, "outer", right)
            down = lax.ppermute(add_down, "outer", left)
        summed = block_of(place).astype(f32) + up.astype(f32) + down.astype(f32)
        return (summed / (no * ni)).astype(bf16)

    middle = width // 512 * 256 if width >= 1024 else width // 2
    grad_weight = jnp.concatenate([reduced(0, middle), reduced(middle, width - middle)], axis=1)

    def share_of(t):
        w_share = lax.dynamic_slice(w_all, (t * half, 0, 0), (half, rows, width))
        return lax.dot_general(
            v_all,
            w_share.reshape(half * rows, width),
            (((1,), (1,)), ((), ())),
            preferred_element_type=f32,
        ).astype(bf16)

    total = 0.0
    for step in list(range(1, nt)) + [0]:
        share = share_of((core + step) % nt)
        if step:
            share = lax.ppermute(share, "tensor", [(k, (k + step) % nt) for k in range(nt)])
        total = total + share.astype(f32)
    total = total.astype(bf16).reshape(ni, tokens, half, rows)
    out = jnp.zeros((tokens, half, ni, rows), bf16)
    for step in range(ni):
        back = (-step) % ni if ni & (ni - 1) else step
        got = total[step] if step == 0 else shifted(total[step], "inter", ni, back)
        source = peer(me, ni, step) if step else me
        out = lax.dynamic_update_slice(out, got[:, :, None, :], (0, 0, source, 0))
    return (out.reshape(tokens, half * ni * rows), grad_weight)


def solution(mesh):
    in_specs = (
        P(("outer", "inter"), None),
        P(("outer", "inter"), "tensor", None, None),
        P(("outer", "inter"), "tensor"),
        P(("outer", "inter"), None),
        P(("outer", "inter"), "tensor"),
    )
    out_specs = (P(("outer", "inter"), "tensor"), P(("outer", "inter"), "tensor"))

    return jax.shard_map(local, mesh=mesh, in_specs=in_specs, out_specs=out_specs, check_vma=False)
```
